32 devices in a mesh: gx: 8 (over z, core), gy: 4 (over y, x).
Axes of the slice: x: 2, y: 2, z: 4, core: 2. Of those that a mesh axis runs over, the one named last changes fastest.
Arguments:
- raw_stack: float32 [2, 32, 128, 2048], P(None, ('gx', 'gy')), may hold values from 0 to 8
- psf_taps: float32 [3, 2, 31], replicated, may hold values from 0.05 to 1
Outputs:
- estimate: float32 [2, 32, 128, 2048], P(None, None, 'gy', 'gx')
The draws below stay inside these ranges and needn't reach their ends.
All inputs are finite; a program needn't handle non-finite values.
Results may differ from the reference program's by a relative error of at most 0.0001.
Values sent between devices are 32-bit elements; how exact they have to be, the bound alone decides.
A program may use at most 192 MiB of HBM per device.

```python
import math
import jax
import jax.numpy as jnp
from jax import lax

CH = 2
NY = 2048
TAPS = 31
ITERS = 2
NX = 128
Z = 32


def draw_raw_stack(key, part):
    key_level = jax.random.fold_in(key, 11)
    key_stripe = jax.random.fold_in(key, 12)
    base_level = jax.random.uniform(key_level, (CH, Z, NX, NY), jnp.float32, 0.25, 4.0)
    stripe_gain = jnp.exp(jax.random.uniform(key_stripe, (CH, Z, 1, NY), jnp.float32, math.log(0.5), math.log(2.0)))
    return base_level * stripe_gain


def setup_inputs(seed: int = 0) -> dict:
    keys = jax.random.split(jax.random.key(seed), 3)
    return {
        "raw_stack": draw_raw_stack(jax.random.fold_in(keys[2], 71), 0),
        "psf_taps": jnp.clip(jnp.exp(jax.random.uniform(keys[1], (3, CH, TAPS), jnp.float32, math.log(0.05), math.log(1.0))), 0.05, 1.0),
    }


BACKGROUND = 0.5
SIGMA_ACROSS = 48.0
SIGMA_ALONG = 96.0


def smoothing_table(length_cells, spread_cells, circular):
    places = lax.iota(jnp.int32, length_cells)
    offset = jnp.abs(places[:, None] - places[None, :])
    if circular:
        offset = jnp.minimum(offset, length_cells - offset)
    scaled = offset.astype(jnp.float32) / spread_cells
    kernel_table = jnp.exp(-0.5 * scaled * scaled)
    return kernel_table / jnp.sum(kernel_table, axis=1, keepdims=True)


def filter_axis(volume, kernel_taps, axis_index):
    half_taps = kernel_taps.shape[1] // 2
    results = []
    for channel in range(volume.shape[0]):
        shifted_axes = jnp.moveaxis(volume[channel], axis_index - 1, -1)
        line_rows = shifted_axes.reshape(-1, 1, shifted_axes.shape[-1])
        kernel = kernel_taps[channel].reshape(1, 1, -1)
        output = lax.conv_general_dilated(line_rows, kernel, (1,), [(half_taps, half_taps)], precision=lax.Precision.HIGHEST)
        results.append(jnp.moveaxis(output.reshape(shifted_axes.shape), -1, axis_index - 1))
    return jnp.stack(results)


def blur_volume(volume, kernel_set):
    result = filter_axis(volume, kernel_set[0], 1)
    result = filter_axis(result, kernel_set[1], 2)
    return filter_axis(result, kernel_set[2], 3)


def reference(raw_stack, psf_taps):
    across_table = smoothing_table(NX, SIGMA_ACROSS, False)
    along_table = smoothing_table(NY, SIGMA_ALONG, True)

    def destripe(plane):
        smoothed = jnp.einsum('ij,cjy->ciy', across_table, plane, precision=lax.Precision.HIGHEST)
        stripes = smoothed - jnp.einsum('cxj,jy->cxy', smoothed, along_table, precision=lax.Precision.HIGHEST)
        return jnp.maximum(plane - stripes, 0.0)

    cleaned = jnp.moveaxis(lax.map(destripe, jnp.moveaxis(raw_stack, 1, 0)), 0, 1)
    forward = psf_taps / jnp.sum(psf_taps, axis=2, keepdims=True)
    backward = forward[:, :, ::-1]
    estimate = cleaned
    for iteration in range(ITERS):
        blurred = blur_volume(estimate, forward)
        ratio_field = cleaned / (blurred + BACKGROUND)
        estimate = estimate * blur_volume(ratio_field, backward)
    return estimate
```

```python
import functools

import jax
import jax.numpy as jnp
from jax import lax
from jax.experimental import pallas as pl
from jax.experimental.pallas import tpu as pltpu
from jax.sharding import PartitionSpec as P

ITERS = 2
BACKGROUND = 0.5
SIGMA_ACROSS = 48.0
SIGMA_ALONG = 96.0
SUB = 8
CHUNKS = 4
MESH = pl.DeviceIdType.MESH


def smoothing_table(length_cells, spread_cells, circular):
    places = lax.iota(jnp.int32, length_cells)
    offset = jnp.abs(places[:, None] - places[None, :])
    if circular:
        offset = jnp.minimum(offset, length_cells - offset)
    scaled = offset.astype(jnp.float32) / spread_cells
    kernel_table = jnp.exp(-0.5 * scaled * scaled)
    return kernel_table / jnp.sum(kernel_table, axis=1, keepdims=True)


def halves(table):
    high = lax.reduce_precision(table, 8, 7)
    return high.astype(jnp.bfloat16), (table - high).astype(jnp.bfloat16)


def banded(taps, lag, mask=None):
    table = jnp.zeros(lag.shape, jnp.float32)
    for k in range(taps.shape[0]):
        hit = lag == k
        table = jnp.where(hit if mask is None else hit & mask, taps[k], table)
    return table


def depth_table(taps, planes):
    size = planes * SUB
    row = lax.broadcasted_iota(jnp.int32, (size, size), 0)
    col = lax.broadcasted_iota(jnp.int32, (size, size), 1)
    lag = col // SUB - row // SUB + taps.shape[0] // 2
    return jnp.concatenate(halves(banded(taps, lag, row % SUB == col % SUB)), axis=0)


def rows_table(taps, lines):
    row = lax.broadcasted_iota(jnp.int32, (lines, lines), 0)
    col = lax.broadcasted_iota(jnp.int32, (lines, lines), 1)
    both = jnp.concatenate(halves(banded(taps, row - col + taps.shape[0] // 2)), axis=1)
    return jnp.concatenate([both, both], axis=0)


def lines_table(taps, cells, edge):
    row = lax.broadcasted_iota(jnp.int32, (cells, cells + 2 * edge), 0)
    col = lax.broadcasted_iota(jnp.int32, (cells, cells + 2 * edge), 1)
    lag = col - row - edge + taps.shape[0] // 2
    return jnp.concatenate(halves(banded(taps, lag)), axis=0)


def split(value):
    high = value.astype(jnp.bfloat16)
    low = (value - high.astype(jnp.float32)).astype(jnp.bfloat16)
    return jnp.concatenate([high, low], axis=1)


def place_of(count_gy, pair, gy):
    first = gy // 2
    along = 2 * first + (gy % 2 + first) % 2
    odd = pair % 2
    return (1 - odd) * along + odd * (count_gy - 1 - along)


def device_of(count_gy, line):
    pair, place = line // count_gy, line % count_gy
    odd = pair % 2
    along = (1 - odd) * place + odd * (count_gy - 1 - place)
    first = along // 2
    return pair, 2 * first + (along % 2 + first) % 2


def deconvolve_kernel(
    count_gx, count_gy, edge, cleaned, depth, rows, lines, out,
    estimate, ratio, wide, stage, send_sem, recv_sem, out_send, out_recv, own_sem,
):
    planes, cells, width = cleaned.shape
    size = planes * SUB
    gx, gy = lax.axis_index("gx"), lax.axis_index("gy")
    pair, core = gx // 2, gx % 2
    place = place_of(count_gy, pair, gy)
    line = pair * count_gy + place
    last = count_gx // 2 * count_gy - 1
    per_gx = count_gy // 2
    lines_x = width // count_gy
    me = gx * count_gy + gy

    barrier = pltpu.get_barrier_semaphore()

    @pl.loop(0, count_gx * count_gy)
    def _(other):
        @pl.when(other != me)
        def _():
            pl.semaphore_signal(
                barrier, inc=1, device_id=(other // count_gy, other % count_gy), device_id_type=MESH
            )

    pl.semaphore_wait(barrier, count_gx * count_gy - 1)

    zeros = jnp.zeros((planes, edge, width), jnp.float32)

    @pl.when(line == 0)
    def _():
        for slot in range(2):
            wide[slot, :, 0:edge, :] = zeros

    @pl.when(line == last)
    def _():
        for slot in range(2):
            wide[slot, :, edge + cells :, :] = zeros

    def edge_copy(slot, up):
        target_pair, target_gy = device_of(count_gy, line + (1 if up else -1))
        source = cells if up else edge
        target = 0 if up else edge + cells
        side = 1 if up else 0
        return pltpu.make_async_remote_copy(
            src_ref=wide.at[slot, :, pl.ds(source, edge), :],
            dst_ref=wide.at[slot, :, pl.ds(target, edge), :],
            send_sem=send_sem.at[slot, side],
            recv_sem=recv_sem.at[slot, side],
            device_id=(target_pair * 2 + core, target_gy),
            device_id_type=MESH,
        )

    def planes_and_rows(field, slot, way, group):
        start = pl.multiple_of(group * SUB, SUB)
        value = field[:, pl.ds(start, SUB), :].reshape(size, width)
        value = jnp.dot(depth[way], split(value), preferred_element_type=jnp.float32)
        value = value[:size] + value[size:]
        value = value[:, :width] + value[:, width:]
        value = jnp.dot(split(value), rows[way], preferred_element_type=jnp.float32)
        value = value[:, :width] + value[:, width:]
        wide[slot, :, pl.ds(edge + start, SUB), :] = value.reshape(planes, SUB, width)

    def along_lines(slot, way, plane):
        value = jnp.dot(lines[way], split(wide[slot, plane]), preferred_element_type=jnp.float32)
        value = value[:cells] + value[cells:]
        return value[:, :width] + value[:, width:]

    def spread(field, slot, way):
        groups = cells // SUB
        outer = edge // SUB

        for group in range(outer):
            planes_and_rows(field, slot, way, group)

        @pl.when(line > 0)
        def _():
            edge_copy(slot, False).start()

        for group in range(groups - outer, groups):
            planes_and_rows(field, slot, way, group)

        @pl.when(line < last)
        def _():
            edge_copy(slot, True).start()

        if groups > 2 * outer:

            @pl.loop(outer, groups - outer)
            def _(group):
                planes_and_rows(field, slot, way, group)

        @pl.when(line > 0)
        def _():
            edge_copy(slot, False).wait_send()
            edge_copy(slot, True).wait_recv()

        @pl.when(line < last)
        def _():
            edge_copy(slot, True).wait_send()
            edge_copy(slot, False).wait_recv()

    def out_copy(chunk, target_gy):
        part = pl.ds(chunk * (planes // CHUNKS), planes // CHUNKS)
        return pltpu.make_async_remote_copy(
            src_ref=stage.at[target_gy, part],
            dst_ref=out.at[core, place % per_gx, part],
            send_sem=out_send.at[chunk, target_gy],
            recv_sem=out_recv.at[chunk, core, place % per_gx],
            device_id=(pair * 2 + place // per_gx, target_gy),
            device_id_type=MESH,
        )

    def own_copy(chunk):
        part = pl.ds(chunk * (planes // CHUNKS), planes // CHUNKS)
        return pltpu.make_async_copy(
            stage.at[gy, part], out.at[core, place % per_gx, part], own_sem.at[chunk]
        )

    def is_own(target_gy):
        return jnp.logical_and(target_gy == gy, place // per_gx == core)

    for iteration in range(ITERS):
        source = cleaned if iteration == 0 else estimate
        spread(source, 0, 0)

        @pl.loop(0, planes, unroll=2)
        def _(plane):
            ratio[plane] = cleaned[plane] / (along_lines(0, 0, plane) + BACKGROUND)

        spread(ratio, 1, 1)
        if iteration < ITERS - 1:

            @pl.loop(0, planes, unroll=2)
            def _(plane):
                estimate[plane] = source[plane] * along_lines(1, 1, plane)

        else:
            for chunk in range(CHUNKS):

                @pl.loop(chunk * (planes // CHUNKS), (chunk + 1) * (planes // CHUNKS), unroll=2)
                def _(plane):
                    value = (source[plane] * along_lines(1, 1, plane)).T
                    for target in range(count_gy):
                        stage[target, plane] = value[target * lines_x : (target + 1) * lines_x]

                for target in range(count_gy):

                    @pl.when(is_own(target))
                    def _():
                        own_copy(chunk).start()

                    @pl.when(jnp.logical_not(is_own(target)))
                    def _():
                        out_copy(chunk, target).start()

    for chunk in range(CHUNKS):
        part = pl.ds(chunk * (planes // CHUNKS), planes // CHUNKS)
        for target in range(count_gy):

            @pl.when(is_own(target))
            def _():
                own_copy(chunk).wait()

            @pl.when(jnp.logical_not(is_own(target)))
            def _():
                out_copy(chunk, target).wait_send()

        for channel in range(2):
            for slot in range(per_gx):
                mine = jnp.logical_and(channel == core, place == core * per_gx + slot)

                @pl.when(jnp.logical_not(mine))
                def _():
                    pltpu.make_async_remote_copy(
                        src_ref=stage.at[0, part],
                        dst_ref=out.at[channel, slot, part],
                        send_sem=out_send.at[chunk, 0],
                        recv_sem=out_recv.at[chunk, channel, slot],
                        device_id=(gx, gy),
                        device_id_type=MESH,
                    ).wait_recv()


def local(raw_stack, psf_taps):
    channels, own_planes, lines_x, lines_y = raw_stack.shape
    half_taps = psf_taps.shape[2] // 2
    count_gx = lax.axis_size("gx")
    count_gy = lax.axis_size("gy")
    pairs = count_gx // channels
    cells = lines_y // (pairs * count_gy)
    planes = own_planes * count_gx * count_gy
    edge = -(-half_taps // SUB) * SUB

    across_table = smoothing_table(lines_x, SIGMA_ACROSS, False)
    along_table = smoothing_table(lines_y, SIGMA_ALONG, True)
    smoothed = jnp.einsum("ij,czjy->cziy", across_table, raw_stack, precision=lax.Precision.HIGH)
    stripes = smoothed - jnp.einsum(
        "czxj,jy->czxy", smoothed, along_table, precision=lax.Precision.HIGH
    )
    cleaned_plane = jnp.maximum(raw_stack - stripes, 0.0)

    blocks = cleaned_plane.reshape(channels, own_planes, lines_x, pairs, count_gy, cells)
    blocks = jnp.transpose(blocks, (3, 0, 4, 1, 5, 2))
    ordered = []
    for pair in range(pairs):
        order = [place_of(count_gy, pair, gy) for gy in range(count_gy)]
        ordered.append(jnp.stack([blocks[pair, :, place] for place in order], axis=1))
    blocks = jnp.stack(ordered).reshape(count_gx * count_gy * own_planes, cells, lines_x)
    cleaned = lax.all_to_all(blocks, ("gx", "gy"), split_axis=0, concat_axis=0, tiled=True)

    channel = lax.axis_index("gx") % channels
    taps = jnp.where(channel == 0, psf_taps[:, 0], psf_taps[:, 1])
    forward = taps / jnp.sum(taps, axis=1, keepdims=True)
    both = (forward, forward[:, ::-1])
    depth = jnp.stack([depth_table(q[0], planes) for q in both])
    rows = jnp.stack([rows_table(q[1], lines_x) for q in both])
    lines = jnp.stack([lines_table(q[2], cells, edge) for q in both])

    per_gx = count_gy // 2
    block_x = lines_x // count_gy
    field = pltpu.VMEM((planes, cells, lines_x), jnp.float32)
    vmem = pl.BlockSpec(memory_space=pltpu.VMEM)
    gathered = pl.pallas_call(
        functools.partial(deconvolve_kernel, count_gx, count_gy, edge),
        out_shape=jax.ShapeDtypeStruct((channels, per_gx, planes, block_x, cells), jnp.float32),
        in_specs=[vmem] * 4,
        out_specs=pl.BlockSpec(memory_space=pl.ANY),
        scratch_shapes=[
            field,
            field,
            pltpu.VMEM((2, planes, cells + 2 * edge, lines_x), jnp.float32),
            pltpu.VMEM((count_gy, planes, block_x, cells), jnp.float32),
            pltpu.SemaphoreType.DMA((2, 2)),
            pltpu.SemaphoreType.DMA((2, 2)),
            pltpu.SemaphoreType.DMA((CHUNKS, count_gy)),
            pltpu.SemaphoreType.DMA((CHUNKS, channels, per_gx)),
            pltpu.SemaphoreType.DMA((CHUNKS,)),
        ],
        compiler_params=pltpu.CompilerParams(
            collective_id=0, has_side_effects=True, vmem_limit_bytes=60 * 1024 * 1024
        ),
    )(cleaned, depth, rows, lines)
    return jnp.transpose(gathered, (0, 2, 3, 1, 4)).reshape(
        channels, planes, block_x, per_gx * cells
    )


def solution(mesh):
    in_specs = (P(None, ("gx", "gy"), None, None), P())
    out_specs = P(None, None, "gy", "gx")
    return jax.shard_map(local, mesh=mesh, in_specs=in_specs, out_specs=out_specs, check_vma=False)
```

```python
import functools

import jax
import jax.numpy as jnp
import numpy as np
from jax import lax
from jax.experimental import pallas as pl
from jax.experimental.pallas import tpu as pltpu
from jax.sharding import PartitionSpec as P

ITERS = 2
BACKGROUND = 0.5
SIGMA_ACROSS = 48.0
SIGMA_ALONG = 96.0
SUB = 8
CHUNKS = 4
MESH = pl.DeviceIdType.MESH


def smoothing_table(length_cells, spread_cells, circular):
    places = lax.iota(jnp.int32, length_cells)
    offset = jnp.abs(places[:, None] - places[None, :])
    if circular:
        offset = jnp.minimum(offset, length_cells - offset)
    scaled = offset.astype(jnp.float32) / spread_cells
    kernel_table = jnp.exp(-0.5 * scaled * scaled)
    return kernel_table / jnp.sum(kernel_table, axis=1, keepdims=True)


def base_row(taps, width, lag_of):
    place = np.arange(width)
    lag = lag_of(np.where(place < width // 2, place, place - width))
    hits = lag[:, None] == np.arange(taps.shape[0])[None, :]
    return jnp.sum(jnp.where(hits, taps[None, :], 0.0), axis=1)


def base_rows(taps, lag_of, reach):
    width = -(-2 * reach // 128) * 128
    return jnp.stack([base_row(q, width, lag_of) for q in taps])[:, None, :]


def shifted(base, start, count, columns):
    block = jnp.broadcast_to(base, (count, base.shape[1]))
    block = pltpu.roll(block, start, 1, stride=1, stride_axis=0)[:, :columns]
    high = block.astype(jnp.bfloat16)
    return high, (block - high.astype(jnp.float32)).astype(jnp.bfloat16)


def tables_kernel(depth_base, rows_base, lines_base, depth, rows, lines):
    size, width, cells = depth.shape[2], rows.shape[1] // 2, lines.shape[1] // 2
    for way in range(2):
        for start in range(0, size, 256):
            high, low = shifted(depth_base[way], start, min(256, size), size)
            depth[way, pl.ds(start, high.shape[0])] = high
            depth[way, pl.ds(size + start, high.shape[0])] = low
        high, low = shifted(rows_base[way], 0, width, width)
        both = jnp.concatenate([high, low], axis=1)
        rows[way] = jnp.concatenate([both, both], axis=0)
        high, low = shifted(lines_base[way], 0, cells, lines.shape[2])
        lines[way] = jnp.concatenate([high, low], axis=0)


def filter_tables(taps, planes, width, cells, edge):
    half = taps.shape[2] // 2
    size = planes * SUB
    depth = base_rows(taps[:, 0], lambda d: np.where(d % SUB == 0, d // SUB + half, -1), size)
    rows = base_rows(taps[:, 1], lambda d: half - d, width)
    lines = base_rows(taps[:, 2], lambda d: d - edge + half, cells + 2 * edge)
    vmem = pl.BlockSpec(memory_space=pltpu.VMEM)
    return pl.pallas_call(
        tables_kernel,
        out_shape=(
            jax.ShapeDtypeStruct((2, 2 * size, size), jnp.bfloat16),
            jax.ShapeDtypeStruct((2, 2 * width, 2 * width), jnp.bfloat16),
            jax.ShapeDtypeStruct((2, 2 * cells, cells + 2 * edge), jnp.bfloat16),
        ),
        in_specs=[vmem] * 3,
        out_specs=[vmem] * 3,
        cost_estimate=pl.CostEstimate(flops=1 << 20, bytes_accessed=1 << 22, transcendentals=0),
    )(depth, rows, lines)


def split(value):
    high = value.astype(jnp.bfloat16)
    low = (value - high.astype(jnp.float32)).astype(jnp.bfloat16)
    return jnp.concatenate([high, low], axis=1)


def place_of(count_gy, pair, gy):
    first = gy // 2
    along = 2 * first + (gy % 2 + first) % 2
    odd = pair % 2
    return (1 - odd) * along + odd * (count_gy - 1 - along)


def device_of(count_gy, line):
    pair, place = line // count_gy, line % count_gy
    odd = pair % 2
    along = (1 - odd) * place + odd * (count_gy - 1 - place)
    first = along // 2
    return pair, 2 * first + (along % 2 + first) % 2


def deconvolve_kernel(
    count_gx, count_gy, edge, cleaned, depth, rows, lines, out,
    estimate, ratio, wide, stage, send_sem, recv_sem, out_send, out_recv, own_sem,
):
    planes, cells, width = cleaned.shape
    size = planes * SUB
    gx, gy = lax.axis_index("gx"), lax.axis_index("gy")
    pair, core = gx // 2, gx % 2
    place = place_of(count_gy, pair, gy)
    line = pair * count_gy + place
    last = count_gx // 2 * count_gy - 1
    per_gx = count_gy // 2
    lines_x = width // count_gy
    me = gx * count_gy + gy

    barrier = pltpu.get_barrier_semaphore()

    @pl.loop(0, count_gx * count_gy)
    def _(other):
        @pl.when(other != me)
        def _():
            pl.semaphore_signal(
                barrier, inc=1, device_id=(other // count_gy, other % count_gy), device_id_type=MESH
            )

    pl.semaphore_wait(barrier, count_gx * count_gy - 1)

    zeros = jnp.zeros((planes, edge, width), jnp.float32)

    @pl.when(line == 0)
    def _():
        for slot in range(2):
            wide[slot, :, 0:edge, :] = zeros

    @pl.when(line == last)
    def _():
        for slot in range(2):
            wide[slot, :, edge + cells :, :] = zeros

    def edge_copy(slot, up):
        target_pair, target_gy = device_of(count_gy, line + (1 if up else -1))
        source = cells if up else edge
        target = 0 if up else edge + cells
        side = 1 if up else 0
        return pltpu.make_async_remote_copy(
            src_ref=wide.at[slot, :, pl.ds(source, edge), :],
            dst_ref=wide.at[slot, :, pl.ds(target, edge), :],
            send_sem=send_sem.at[slot, side],
            recv_sem=recv_sem.at[slot, side],
            device_id=(target_pair * 2 + core, target_gy),
            device_id_type=MESH,
        )

    def planes_and_rows(field, slot, way, group):
        start = pl.multiple_of(group * SUB, SUB)
        value = field[:, pl.ds(start, SUB), :].reshape(size, width)
        value = jnp.dot(depth[way], split(value), preferred_element_type=jnp.float32)
        value = value[:size] + value[size:]
        value = value[:, :width] + value[:, width:]
        value = jnp.dot(split(value), rows[way], preferred_element_type=jnp.float32)
        value = value[:, :width] + value[:, width:]
        wide[slot, :, pl.ds(edge + start, SUB), :] = value.reshape(planes, SUB, width)

    def along_lines(slot, way, plane):
        value = jnp.dot(lines[way], split(wide[slot, plane]), preferred_element_type=jnp.float32)
        value = value[:cells] + value[cells:]
        return value[:, :width] + value[:, width:]

    def spread(field, slot, way):
        groups = cells // SUB
        outer = edge // SUB

        @pl.loop(0, 2 * outer, unroll=2)
        def _(step):
            planes_and_rows(field, slot, way, lax.rem(step + groups - outer, groups))

        @pl.when(line > 0)
        def _():
            edge_copy(slot, False).start()

        @pl.when(line < last)
        def _():
            edge_copy(slot, True).start()

        if groups > 2 * outer:

            @pl.loop(outer, groups - outer, unroll=4 if groups % 4 == 0 else 1)
            def _(group):
                planes_and_rows(field, slot, way, group)

        @pl.when(line > 0)
        def _():
            edge_copy(slot, False).wait_send()
            edge_copy(slot, True).wait_recv()

        @pl.when(line < last)
        def _():
            edge_copy(slot, True).wait_send()
            edge_copy(slot, False).wait_recv()

    def out_copy(chunk, target_gy):
        part = pl.ds(chunk * (planes // CHUNKS), planes // CHUNKS)
        return pltpu.make_async_remote_copy(
            src_ref=stage.at[target_gy, part],
            dst_ref=out.at[core, place % per_gx, part],
            send_sem=out_send.at[chunk, target_gy],
            recv_sem=out_recv.at[chunk, core, place % per_gx],
            device_id=(pair * 2 + place // per_gx, target_gy),
            device_id_type=MESH,
        )

    def own_copy(chunk):
        part = pl.ds(chunk * (planes // CHUNKS), planes // CHUNKS)
        return pltpu.make_async_copy(
            stage.at[gy, part], out.at[core, place % per_gx, part], own_sem.at[chunk]
        )

    def is_own(target_gy):
        return jnp.logical_and(target_gy == gy, place // per_gx == core)

    for iteration in range(ITERS):
        source = cleaned if iteration == 0 else estimate
        spread(source, 0, 0)

        @pl.loop(0, planes, unroll=4)
        def _(plane):
            ratio[plane] = cleaned[plane] / (along_lines(0, 0, plane) + BACKGROUND)

        spread(ratio, 1, 1)
        if iteration < ITERS - 1:

            @pl.loop(0, planes, unroll=4)
            def _(plane):
                estimate[plane] = source[plane] * along_lines(1, 1, plane)

        else:
            for chunk in range(CHUNKS):

                @pl.loop(chunk * (planes // CHUNKS), (chunk + 1) * (planes // CHUNKS), unroll=4)
                def _(plane):
                    value = (source[plane] * along_lines(1, 1, plane)).T
                    for target in range(count_gy):
                        stage[target, plane] = value[target * lines_x : (target + 1) * lines_x]

                for target in range(count_gy):

                    @pl.when(is_own(target))
                    def _():
                        own_copy(chunk).start()

                    @pl.when(jnp.logical_not(is_own(target)))
                    def _():
                        out_copy(chunk, target).start()

    for chunk in range(CHUNKS):
        part = pl.ds(chunk * (planes // CHUNKS), planes // CHUNKS)
        for target in range(count_gy):

            @pl.when(is_own(target))
            def _():
                own_copy(chunk).wait()

            @pl.when(jnp.logical_not(is_own(target)))
            def _():
                out_copy(chunk, target).wait_send()

        for channel in range(2):
            for slot in range(per_gx):
                mine = jnp.logical_and(channel == core, place == core * per_gx + slot)

                @pl.when(jnp.logical_not(mine))
                def _():
                    pltpu.make_async_remote_copy(
                        src_ref=stage.at[0, part],
                        dst_ref=out.at[channel, slot, part],
                        send_sem=out_send.at[chunk, 0],
                        recv_sem=out_recv.at[chunk, channel, slot],
                        device_id=(gx, gy),
                        device_id_type=MESH,
                    ).wait_recv()


def local(raw_stack, psf_taps):
    channels, own_planes, lines_x, lines_y = raw_stack.shape
    half_taps = psf_taps.shape[2] // 2
    count_gx = lax.axis_size("gx")
    count_gy = lax.axis_size("gy")
    pairs = count_gx // channels
    cells = lines_y // (pairs * count_gy)
    planes = own_planes * count_gx * count_gy
    edge = -(-half_taps // SUB) * SUB

    across_table = smoothing_table(lines_x, SIGMA_ACROSS, False)
    along_table = smoothing_table(lines_y, SIGMA_ALONG, True)
    smoothed = jnp.einsum("ij,czjy->cziy", across_table, raw_stack, precision=lax.Precision.HIGH)
    stripes = smoothed - jnp.einsum(
        "czxj,jy->czxy", smoothed, along_table, precision=lax.Precision.HIGH
    )
    cleaned_plane = jnp.maximum(raw_stack - stripes, 0.0)

    blocks = cleaned_plane.reshape(channels, own_planes, lines_x, pairs, count_gy, cells)
    blocks = jnp.transpose(blocks, (3, 0, 4, 1, 5, 2))
    ordered = []
    for pair in range(pairs):
        order = [place_of(count_gy, pair, gy) for gy in range(count_gy)]
        ordered.append(jnp.stack([blocks[pair, :, place] for place in order], axis=1))
    blocks = jnp.stack(ordered).reshape(count_gx * count_gy * own_planes, cells, lines_x)
    cleaned = lax.all_to_all(blocks, ("gx", "gy"), split_axis=0, concat_axis=0, tiled=True)

    channel = lax.axis_index("gx") % channels
    taps = jnp.where(channel == 0, psf_taps[:, 0], psf_taps[:, 1])
    forward = taps / jnp.sum(taps, axis=1, keepdims=True)
    both = jnp.stack([forward, forward[:, ::-1]])
    depth, rows, lines = filter_tables(both, planes, lines_x, cells, edge)

    per_gx = count_gy // 2
    block_x = lines_x // count_gy
    field = pltpu.VMEM((planes, cells, lines_x), jnp.float32)
    vmem = pl.BlockSpec(memory_space=pltpu.VMEM)
    gathered = pl.pallas_call(
        functools.partial(deconvolve_kernel, count_gx, count_gy, edge),
        out_shape=jax.ShapeDtypeStruct((channels, per_gx, planes, block_x, cells), jnp.float32),
        in_specs=[vmem] * 4,
        out_specs=pl.BlockSpec(memory_space=pl.ANY),
        scratch_shapes=[
            field,
            field,
            pltpu.VMEM((2, planes, cells + 2 * edge, lines_x), jnp.float32),
            pltpu.VMEM((count_gy, planes, block_x, cells), jnp.float32),
            pltpu.SemaphoreType.DMA((2, 2)),
            pltpu.SemaphoreType.DMA((2, 2)),
            pltpu.SemaphoreType.DMA((CHUNKS, count_gy)),
            pltpu.SemaphoreType.DMA((CHUNKS, channels, per_gx)),
            pltpu.SemaphoreType.DMA((CHUNKS,)),
        ],
        compiler_params=pltpu.CompilerParams(
            collective_id=0, has_side_effects=True, vmem_limit_bytes=60 * 1024 * 1024
        ),
    )(cleaned, depth, rows, lines)
    return jnp.transpose(gathered, (0, 2, 3, 1, 4)).reshape(
        channels, planes, block_x, per_gx * cells
    )


def solution(mesh):
    in_specs = (P(None, ("gx", "gy"), None, None), P())
    out_specs = P(None, None, "gy", "gx")
    return jax.shard_map(local, mesh=mesh, in_specs=in_specs, out_specs=out_specs, check_vma=False)
```

```python
import functools

import jax
import jax.numpy as jnp
import numpy as np
from jax import lax
from jax.experimental import pallas as pl
from jax.experimental.pallas import tpu as pltpu
from jax.sharding import PartitionSpec as P

ITERS = 2
BACKGROUND = 0.5
SIGMA_ACROSS = 48.0
SIGMA_ALONG = 96.0
SUB = 8
CHUNKS = 4
MESH = pl.DeviceIdType.MESH


def smoothing_table(length_cells, spread_cells):
    places = lax.iota(jnp.int32, length_cells)
    offset = jnp.abs(places[:, None] - places[None, :])
    scaled = offset.astype(jnp.float32) / spread_cells
    kernel_table = jnp.exp(-0.5 * scaled * scaled)
    return kernel_table / jnp.sum(kernel_table, axis=1, keepdims=True)


def circular_row(length_cells, spread_cells):
    places = lax.broadcasted_iota(jnp.int32, (1, length_cells), 1)
    scaled = jnp.minimum(places, length_cells - places).astype(jnp.float32) / spread_cells
    kernel_row = jnp.exp(-0.5 * scaled * scaled)
    return kernel_row / jnp.sum(kernel_row)


def base_row(taps, width, lag_of):
    place = np.arange(width)
    lag = lag_of(np.where(place < width // 2, place, place - width))
    hits = lag[:, None] == np.arange(taps.shape[0])[None, :]
    return jnp.sum(jnp.where(hits, taps[None, :], 0.0), axis=1)


def base_rows(taps, lag_of, reach):
    width = -(-2 * reach // 128) * 128
    return jnp.stack([base_row(q, width, lag_of) for q in taps])[:, None, :]


def shifted(base, start, count, columns):
    block = jnp.broadcast_to(base, (count, base.shape[1]))
    block = pltpu.roll(block, start, 1, stride=1, stride_axis=0)[:, :columns]
    high = block.astype(jnp.bfloat16)
    return high, (block - high.astype(jnp.float32)).astype(jnp.bfloat16)


def fill_tables(depth_base, rows_base, lines_base, depth, rows, lines):
    size, width, cells = depth.shape[2], rows.shape[1] // 2, lines.shape[1] // 2
    for way in range(2):
        for start in range(0, size, 256):
            high, low = shifted(depth_base[way], start, min(256, size), size)
            depth[way, pl.ds(start, high.shape[0])] = high
            depth[way, pl.ds(size + start, high.shape[0])] = low
        high, low = shifted(rows_base[way], 0, width, width)
        both = jnp.concatenate([high, low], axis=1)
        rows[way] = jnp.concatenate([both, both], axis=0)
        high, low = shifted(lines_base[way], 0, cells, lines.shape[2])
        lines[way] = jnp.concatenate([high, low], axis=0)


def split(value):
    high = value.astype(jnp.bfloat16)
    low = (value - high.astype(jnp.float32)).astype(jnp.bfloat16)
    return jnp.concatenate([high, low], axis=1)


def place_of(count_gy, pair, gy):
    first = gy // 2
    along = 2 * first + (gy % 2 + first) % 2
    odd = pair % 2
    return (1 - odd) * along + odd * (count_gy - 1 - along)


def device_of(count_gy, line):
    pair, place = line // count_gy, line % count_gy
    odd = pair % 2
    along = (1 - odd) * place + odd * (count_gy - 1 - place)
    first = along // 2
    return pair, 2 * first + (along % 2 + first) % 2


def deconvolve_kernel(
    count_gx, count_gy, edge, raw, across, along_base, depth_base, rows_base, lines_base, out,
    cleaned, estimate, ratio, wide, stage, along, smooth, depth, rows, lines,
    held, send_sem, recv_sem, out_send, out_recv, own_sem, plane_send, plane_recv, held_sem,
):
    planes, cells, width = cleaned.shape
    size = planes * SUB
    gx, gy = lax.axis_index("gx"), lax.axis_index("gy")
    pair, core = gx // 2, gx % 2
    place = place_of(count_gy, pair, gy)
    line = pair * count_gy + place
    last = count_gx // 2 * count_gy - 1
    per_gx = count_gy // 2
    lines_x = width // count_gy
    me = gx * count_gy + gy

    def load(channel):
        return pltpu.make_async_copy(raw.at[channel, 0], held, held_sem)

    load(0).start()
    barrier = pltpu.get_barrier_semaphore()

    @pl.loop(0, count_gx * count_gy)
    def _(other):
        @pl.when(other != me)
        def _():
            pl.semaphore_signal(
                barrier, inc=1, device_id=(other // count_gy, other % count_gy), device_id_type=MESH
            )

    channels, _, _, lines_y = raw.shape
    block = along.shape[0] // 2
    blocks = lines_y // block
    chunks = lines_y // cells
    per_block = block // cells
    high, low = shifted(along_base[...], 0, block, lines_y)
    along[0:block] = high
    along[block : 2 * block] = low

    def smooth_block(index):
        columns = pl.ds(pl.multiple_of(index * block, block), block)
        value = held[:, columns]
        high = value.astype(jnp.bfloat16)
        low = (value - high.astype(jnp.float32)).astype(jnp.bfloat16)
        product = jnp.dot(across[...], high, preferred_element_type=jnp.float32)
        total = product[:width] + product[width:]
        total += jnp.dot(across[0:width], low, preferred_element_type=jnp.float32)
        high = total.astype(jnp.bfloat16)
        smooth[0:width, columns] = high
        smooth[width : 2 * width, columns] = (total - high.astype(jnp.float32)).astype(jnp.bfloat16)

    def clean_block(channel, index):
        total = jnp.zeros((width, block), jnp.float32)
        for other in range(blocks):
            columns = pl.ds(other * block, block)
            shift = lax.rem(index - other + blocks, blocks)
            table = pl.ds(pl.multiple_of(shift * block, block), block)
            product = jnp.dot(
                smooth[:, columns], along[0:block, table], preferred_element_type=jnp.float32
            )
            total += product[:width] + product[width:]
            total += jnp.dot(
                smooth[0:width, columns], along[block : 2 * block, table],
                preferred_element_type=jnp.float32,
            )
        columns = pl.ds(pl.multiple_of(index * block, block), block)
        smoothed = smooth[0:width, columns].astype(jnp.float32)
        smoothed += smooth[width : 2 * width, columns].astype(jnp.float32)
        value = jnp.maximum(held[:, columns] - (smoothed - total), 0.0)
        estimate[pl.ds(channel * chunks + index * per_block, per_block)] = value.T.reshape(
            per_block, cells, width
        )

    def plane_copy(channel, chunk):
        target_pair, target_gy = device_of(count_gy, chunk)
        return pltpu.make_async_remote_copy(
            src_ref=estimate.at[channel * chunks + chunk],
            dst_ref=cleaned.at[me],
            send_sem=plane_send.at[channel * chunks + chunk],
            recv_sem=plane_recv.at[me],
            device_id=(target_pair * 2 + channel, target_gy),
            device_id_type=MESH,
        )

    own_plane = pltpu.make_async_copy(
        estimate.at[core * chunks + line], cleaned.at[me], plane_send.at[core * chunks + line]
    )

    def is_own_plane(channel, chunk):
        return jnp.logical_and(channel == core, chunk == line)

    for channel in range(channels):
        if channel > 0:
            load(channel).start()
        load(channel).wait()

        @pl.loop(0, blocks, unroll=2)
        def _(index):
            smooth_block(index)

        if channel == 0:
            pl.semaphore_wait(barrier, count_gx * count_gy - 1)

        @pl.loop(0, blocks)
        def _(step):
            index = lax.rem(step + (line + 1) // per_block + blocks // 2, blocks)
            clean_block(channel, index)
            for part in range(per_block):
                chunk = index * per_block + part

                @pl.when(is_own_plane(channel, chunk))
                def _():
                    own_plane.start()

                @pl.when(jnp.logical_not(is_own_plane(channel, chunk)))
                def _():
                    plane_copy(channel, chunk).start()

    fill_tables(depth_base, rows_base, lines_base, depth, rows, lines)

    zeros = jnp.zeros((planes, edge, width), jnp.float32)

    @pl.when(line == 0)
    def _():
        for slot in range(2):
            wide[slot, :, 0:edge, :] = zeros

    @pl.when(line == last)
    def _():
        for slot in range(2):
            wide[slot, :, edge + cells :, :] = zeros

    own_plane.wait()
    for channel in range(channels):

        @pl.loop(0, chunks)
        def _(chunk):
            @pl.when(jnp.logical_not(is_own_plane(channel, chunk)))
            def _():
                plane_copy(channel, chunk).wait_send()

    @pl.loop(0, count_gx * count_gy)
    def _(other):
        @pl.when(other != me)
        def _():
            pltpu.make_async_remote_copy(
                src_ref=estimate.at[0],
                dst_ref=cleaned.at[other],
                send_sem=plane_send.at[0],
                recv_sem=plane_recv.at[other],
                device_id=(gx, gy),
                device_id_type=MESH,
            ).wait_recv()

    def edge_copy(slot, up):
        target_pair, target_gy = device_of(count_gy, line + (1 if up else -1))
        source = cells if up else edge
        target = 0 if up else edge + cells
        side = 1 if up else 0
        return pltpu.make_async_remote_copy(
            src_ref=wide.at[slot, :, pl.ds(source, edge), :],
            dst_ref=wide.at[slot, :, pl.ds(target, edge), :],
            send_sem=send_sem.at[slot, side],
            recv_sem=recv_sem.at[slot, side],
            device_id=(target_pair * 2 + core, target_gy),
            device_id_type=MESH,
        )

    def planes_and_rows(field, slot, way, group):
        start = pl.multiple_of(group * SUB, SUB)
        value = field[:, pl.ds(start, SUB), :].reshape(size, width)
        value = jnp.dot(depth[way], split(value), preferred_element_type=jnp.float32)
        value = value[:size] + value[size:]
        value = value[:, :width] + value[:, width:]
        value = jnp.dot(split(value), rows[way], preferred_element_type=jnp.float32)
        value = value[:, :width] + value[:, width:]
        wide[slot, :, pl.ds(edge + start, SUB), :] = value.reshape(planes, SUB, width)

    def along_lines(slot, way, plane):
        value = jnp.dot(lines[way], split(wide[slot, plane]), preferred_element_type=jnp.float32)
        value = value[:cells] + value[cells:]
        return value[:, :width] + value[:, width:]

    def spread(field, slot, way):
        groups = cells // SUB
        outer = edge // SUB

        @pl.loop(0, 2 * outer, unroll=2)
        def _(step):
            planes_and_rows(field, slot, way, lax.rem(step + groups - outer, groups))

        @pl.when(line > 0)
        def _():
            edge_copy(slot, False).start()

        @pl.when(line < last)
        def _():
            edge_copy(slot, True).start()

        if groups > 2 * outer:

            @pl.loop(outer, groups - outer, unroll=4 if groups % 4 == 0 else 1)
            def _(group):
                planes_and_rows(field, slot, way, group)

        @pl.when(line > 0)
        def _():
            edge_copy(slot, False).wait_send()
            edge_copy(slot, True).wait_recv()

        @pl.when(line < last)
        def _():
            edge_copy(slot, True).wait_send()
            edge_copy(slot, False).wait_recv()

    def out_copy(chunk, target_gy):
        part = pl.ds(chunk * (planes // CHUNKS), planes // CHUNKS)
        return pltpu.make_async_remote_copy(
            src_ref=stage.at[target_gy, part],
            dst_ref=out.at[core, place % per_gx, part],
            send_sem=out_send.at[chunk, target_gy],
            recv_sem=out_recv.at[chunk, core, place % per_gx],
            device_id=(pair * 2 + place // per_gx, target_gy),
            device_id_type=MESH,
        )

    def own_copy(chunk):
        part = pl.ds(chunk * (planes // CHUNKS), planes // CHUNKS)
        return pltpu.make_async_copy(
            stage.at[gy, part], out.at[core, place % per_gx, part], own_sem.at[chunk]
        )

    def is_own(target_gy):
        return jnp.logical_and(target_gy == gy, place // per_gx == core)

    for iteration in range(ITERS):
        source = cleaned if iteration == 0 else estimate
        spread(source, 0, 0)

        @pl.loop(0, planes, unroll=4)
        def _(plane):
            ratio[plane] = cleaned[plane] / (along_lines(0, 0, plane) + BACKGROUND)

        spread(ratio, 1, 1)
        if iteration < ITERS - 1:

            @pl.loop(0, planes, unroll=4)
            def _(plane):
                estimate[plane] = source[plane] * along_lines(1, 1, plane)

        else:
            for chunk in range(CHUNKS):

                @pl.loop(chunk * (planes // CHUNKS), (chunk + 1) * (planes // CHUNKS), unroll=4)
                def _(plane):
                    value = (source[plane] * along_lines(1, 1, plane)).T
                    for target in range(count_gy):
                        stage[target, plane] = value[target * lines_x : (target + 1) * lines_x]

                for target in range(count_gy):

                    @pl.when(is_own(target))
                    def _():
                        own_copy(chunk).start()

                    @pl.when(jnp.logical_not(is_own(target)))
                    def _():
                        out_copy(chunk, target).start()

    for chunk in range(CHUNKS):
        part = pl.ds(chunk * (planes // CHUNKS), planes // CHUNKS)
        for target in range(count_gy):

            @pl.when(is_own(target))
            def _():
                own_copy(chunk).wait()

            @pl.when(jnp.logical_not(is_own(target)))
            def _():
                out_copy(chunk, target).wait_send()

        for channel in range(2):
            for slot in range(per_gx):
                mine = jnp.logical_and(channel == core, place == core * per_gx + slot)

                @pl.when(jnp.logical_not(mine))
                def _():
                    pltpu.make_async_remote_copy(
                        src_ref=stage.at[0, part],
                        dst_ref=out.at[channel, slot, part],
                        send_sem=out_send.at[chunk, 0],
                        recv_sem=out_recv.at[chunk, channel, slot],
                        device_id=(gx, gy),
                        device_id_type=MESH,
                    ).wait_recv()


def local(raw_stack, psf_taps):
    channels, own_planes, lines_x, lines_y = raw_stack.shape
    half_taps = psf_taps.shape[2] // 2
    count_gx = lax.axis_size("gx")
    count_gy = lax.axis_size("gy")
    pairs = count_gx // channels
    cells = lines_y // (pairs * count_gy)
    planes = own_planes * count_gx * count_gy
    edge = -(-half_taps // SUB) * SUB

    across_table = smoothing_table(lines_x, SIGMA_ACROSS)
    high = lax.reduce_precision(across_table, 8, 7)
    across = jnp.concatenate([high, across_table - high], axis=0).astype(jnp.bfloat16)
    along_base = circular_row(lines_y, SIGMA_ALONG)
    block = min(lines_y, 256)

    channel = lax.axis_index("gx") % channels
    taps = jnp.where(channel == 0, psf_taps[:, 0], psf_taps[:, 1])
    forward = taps / jnp.sum(taps, axis=1, keepdims=True)
    both = jnp.stack([forward, forward[:, ::-1]])
    size = planes * SUB
    depth = base_rows(
        both[:, 0], lambda d: np.where(d % SUB == 0, d // SUB + half_taps, -1), size
    )
    rows = base_rows(both[:, 1], lambda d: half_taps - d, lines_x)
    lines = base_rows(both[:, 2], lambda d: d - edge + half_taps, cells + 2 * edge)

    per_gx = count_gy // 2
    block_x = lines_x // count_gy
    field = pltpu.VMEM((planes, cells, lines_x), jnp.float32)
    vmem = pl.BlockSpec(memory_space=pltpu.VMEM)
    gathered = pl.pallas_call(
        functools.partial(deconvolve_kernel, count_gx, count_gy, edge),
        out_shape=jax.ShapeDtypeStruct((channels, per_gx, planes, block_x, cells), jnp.float32),
        in_specs=[pl.BlockSpec(memory_space=pl.ANY)] + [vmem] * 5,
        out_specs=pl.BlockSpec(memory_space=pl.ANY),
        scratch_shapes=[
            field,
            field,
            field,
            pltpu.VMEM((2, planes, cells + 2 * edge, lines_x), jnp.float32),
            pltpu.VMEM((count_gy, planes, block_x, cells), jnp.float32),
            pltpu.VMEM((2 * block, lines_y), jnp.bfloat16),
            pltpu.VMEM((2 * lines_x, lines_y), jnp.bfloat16),
            pltpu.VMEM((2, 2 * size, size), jnp.bfloat16),
            pltpu.VMEM((2, 2 * lines_x, 2 * lines_x), jnp.bfloat16),
            pltpu.VMEM((2, 2 * cells, cells + 2 * edge), jnp.bfloat16),
            pltpu.VMEM((lines_x, lines_y), jnp.float32),
            pltpu.SemaphoreType.DMA((2, 2)),
            pltpu.SemaphoreType.DMA((2, 2)),
            pltpu.SemaphoreType.DMA((CHUNKS, count_gy)),
            pltpu.SemaphoreType.DMA((CHUNKS, channels, per_gx)),
            pltpu.SemaphoreType.DMA((CHUNKS,)),
            pltpu.SemaphoreType.DMA((planes,)),
            pltpu.SemaphoreType.DMA((planes,)),
            pltpu.SemaphoreType.DMA,
        ],
        compiler_params=pltpu.CompilerParams(
            collective_id=0, has_side_effects=True, vmem_limit_bytes=67043328
        ),
    )(raw_stack, across, along_base, depth, rows, lines)
    return jnp.transpose(gathered, (0, 2, 3, 1, 4)).reshape(
        channels, planes, block_x, per_gx * cells
    )


def solution(mesh):
    in_specs = (P(None, ("gx", "gy"), None, None), P())
    out_specs = P(None, None, "gy", "gx")
    return jax.shard_map(local, mesh=mesh, in_specs=in_specs, out_specs=out_specs, check_vma=False)
```

```python
import functools

import jax
import jax.numpy as jnp
from jax import lax
from jax.experimental import pallas as pl
from jax.experimental.pallas import tpu as pltpu
from jax.sharding import PartitionSpec as P

ITERS = 2
BACKGROUND = 0.5
SIGMA_ACROSS = 48.0
SIGMA_ALONG = 96.0
SUB = 8
CHUNKS = 4
MESH = pl.DeviceIdType.MESH


def smoothing_table(length_cells, spread_cells):
    rows = lax.broadcasted_iota(jnp.int32, (length_cells, length_cells), 0)
    columns = lax.broadcasted_iota(jnp.int32, (length_cells, length_cells), 1)
    scaled = (rows - columns).astype(jnp.float32) / spread_cells
    kernel_table = jnp.exp(-0.5 * scaled * scaled)
    return kernel_table / jnp.sum(kernel_table, axis=1, keepdims=True)


def circular_row(length_cells, spread_cells):
    places = lax.broadcasted_iota(jnp.int32, (1, length_cells), 1)
    scaled = jnp.minimum(places, length_cells - places).astype(jnp.float32) / spread_cells
    kernel_row = jnp.exp(-0.5 * scaled * scaled)
    return kernel_row / jnp.sum(kernel_row, axis=1, keepdims=True)


def base_rows(taps, axis, channel, reach, lag_of):
    count = taps.shape[2]
    width = -(-2 * reach // 128) * 128
    place = lax.broadcasted_iota(jnp.int32, (1, width), 1)
    lag = lag_of(jnp.where(place < width // 2, place, place - width))
    forward = jnp.zeros((1, width), jnp.float32)
    backward = forward
    total = forward
    for k in range(count):
        tap = taps[axis, channel, k]
        total = total + tap
        forward = jnp.where(lag == k, tap, forward)
        backward = jnp.where(lag == count - 1 - k, tap, backward)
    return forward / total, backward / total


def shifted(base, start, count, columns):
    block = jnp.broadcast_to(base, (count, base.shape[1]))
    block = pltpu.roll(block, start, 1, stride=1, stride_axis=0)[:, :columns]
    high = block.astype(jnp.bfloat16)
    return high, (block - high.astype(jnp.float32)).astype(jnp.bfloat16)


def fill_tables(taps, channel, edge, cells, depth, rows, middle, ends):
    size, width = depth.shape[2], rows.shape[1] // 2
    half = taps.shape[2] // 2
    depth_base = base_rows(
        taps, 0, channel, size,
        lambda d: jnp.where((d & (SUB - 1)) == 0, (d >> (SUB.bit_length() - 1)) + half, -1),
    )
    rows_base = base_rows(taps, 1, channel, width, lambda d: half - d)
    lines_base = base_rows(taps, 2, channel, max(cells, 3 * edge), lambda d: d - edge + half)
    for way in range(2):
        for start in range(0, size, 256):
            high, low = shifted(depth_base[way], start, min(256, size), size)
            depth[way, pl.ds(start, high.shape[0])] = high
            depth[way, pl.ds(size + start, high.shape[0])] = low
        high, low = shifted(rows_base[way], 0, width, width)
        both = jnp.concatenate([high, low], axis=1)
        rows[way] = jnp.concatenate([both, both], axis=0)
        if cells > 2 * edge:
            high, low = shifted(lines_base[way], 0, cells - 2 * edge, cells)
            middle[way] = jnp.concatenate([high, low], axis=0)
        high, low = shifted(lines_base[way], 0, edge, 3 * edge)
        ends[way] = jnp.concatenate([high, low], axis=0)


def split(value):
    high = value.astype(jnp.bfloat16)
    low = (value - high.astype(jnp.float32)).astype(jnp.bfloat16)
    return jnp.concatenate([high, low], axis=1)


def place_of(count_gy, pair, gy):
    first = gy // 2
    along = 2 * first + (gy % 2 + first) % 2
    odd = pair % 2
    return (1 - odd) * along + odd * (count_gy - 1 - along)


def device_of(count_gy, line):
    pair, place = line // count_gy, line % count_gy
    odd = pair % 2
    along = (1 - odd) * place + odd * (count_gy - 1 - place)
    first = along // 2
    return pair, 2 * first + (along % 2 + first) % 2


def deconvolve_kernel(
    count_gx, count_gy, edge, raw, taps, out,
    cleaned, estimate, ratio, wide, stage, along, smooth, across, depth, rows, middle, ends,
    held, send_sem, recv_sem, out_send, out_recv, own_sem, plane_send, plane_recv, held_sem,
):
    planes, cells, width = cleaned.shape
    size = planes * SUB
    gx, gy = lax.axis_index("gx"), lax.axis_index("gy")
    pair, core = gx // 2, gx % 2
    place = place_of(count_gy, pair, gy)
    line = pair * count_gy + place
    last = count_gx // 2 * count_gy - 1
    per_gx = count_gy // 2
    lines_x = width // count_gy
    me = gx * count_gy + gy

    def load(channel):
        return pltpu.make_async_copy(raw.at[channel, 0], held, held_sem)

    load(0).start()
    barrier = pltpu.get_barrier_semaphore()

    @pl.loop(0, count_gx * count_gy)
    def _(other):
        @pl.when(other != me)
        def _():
            pl.semaphore_signal(
                barrier, inc=1, device_id=(other // count_gy, other % count_gy), device_id_type=MESH
            )

    channels, _, _, lines_y = raw.shape
    block = along.shape[0] // 2
    blocks = lines_y // block
    chunks = lines_y // cells
    per_block = block // cells
    table = smoothing_table(width, SIGMA_ACROSS)
    high = table.astype(jnp.bfloat16)
    across[0:width] = high
    across[width : 2 * width] = (table - high.astype(jnp.float32)).astype(jnp.bfloat16)
    high, low = shifted(circular_row(lines_y, SIGMA_ALONG), 0, block, lines_y)
    along[0:block] = high
    along[block : 2 * block] = low

    def smooth_block(index):
        columns = pl.ds(pl.multiple_of(index * block, block), block)
        value = held[:, columns]
        high = value.astype(jnp.bfloat16)
        low = (value - high.astype(jnp.float32)).astype(jnp.bfloat16)
        product = jnp.dot(across[...], high, preferred_element_type=jnp.float32)
        total = product[:width] + product[width:]
        total += jnp.dot(across[0:width], low, preferred_element_type=jnp.float32)
        high = total.astype(jnp.bfloat16)
        smooth[0:width, columns] = high
        smooth[width : 2 * width, columns] = (total - high.astype(jnp.float32)).astype(jnp.bfloat16)

    def clean_block(channel, index):
        total = jnp.zeros((width, block), jnp.float32)
        for other in range(blocks):
            columns = pl.ds(other * block, block)
            shift = lax.rem(index - other + blocks, blocks)
            table = pl.ds(pl.multiple_of(shift * block, block), block)
            product = jnp.dot(
                smooth[:, columns], along[0:block, table], preferred_element_type=jnp.float32
            )
            total += product[:width] + product[width:]
            total += jnp.dot(
                smooth[0:width, columns], along[block : 2 * block, table],
                preferred_element_type=jnp.float32,
            )
        columns = pl.ds(pl.multiple_of(index * block, block), block)
        smoothed = smooth[0:width, columns].astype(jnp.float32)
        smoothed += smooth[width : 2 * width, columns].astype(jnp.float32)
        value = jnp.maximum(held[:, columns] - (smoothed - total), 0.0)
        estimate[pl.ds(channel * chunks + index * per_block, per_block)] = value.T.reshape(
            per_block, cells, width
        )

    def plane_copy(channel, chunk):
        target_pair, target_gy = device_of(count_gy, chunk)
        return pltpu.make_async_remote_copy(
            src_ref=estimate.at[channel * chunks + chunk],
            dst_ref=cleaned.at[me],
            send_sem=plane_send.at[channel * chunks + chunk],
            recv_sem=plane_recv.at[me],
            device_id=(target_pair * 2 + channel, target_gy),
            device_id_type=MESH,
        )

    own_plane = pltpu.make_async_copy(
        estimate.at[core * chunks + line], cleaned.at[me], plane_send.at[core * chunks + line]
    )

    def is_own_plane(channel, chunk):
        return jnp.logical_and(channel == core, chunk == line)

    for channel in range(channels):
        if channel > 0:
            load(channel).start()
        load(channel).wait()

        @pl.loop(0, blocks, unroll=2)
        def _(index):
            smooth_block(index)

        if channel == 0:
            pl.semaphore_wait(barrier, count_gx * count_gy - 1)

        @pl.loop(0, blocks)
        def _(step):
            index = lax.rem(step + (line + 1) // per_block + blocks // 2, blocks)
            clean_block(channel, index)
            for part in range(per_block):
                chunk = index * per_block + part

                @pl.when(is_own_plane(channel, chunk))
                def _():
                    own_plane.start()

                @pl.when(jnp.logical_not(is_own_plane(channel, chunk)))
                def _():
                    plane_copy(channel, chunk).start()

    fill_tables(taps, core, edge, cells, depth, rows, middle, ends)

    zeros = jnp.zeros((planes, edge, width), jnp.float32)

    @pl.when(line == 0)
    def _():
        for slot in range(2):
            wide[slot, :, 0:edge, :] = zeros

    @pl.when(line == last)
    def _():
        for slot in range(2):
            wide[slot, :, edge + cells :, :] = zeros

    own_plane.wait()
    for channel in range(channels):

        @pl.loop(0, chunks)
        def _(chunk):
            @pl.when(jnp.logical_not(is_own_plane(channel, chunk)))
            def _():
                plane_copy(channel, chunk).wait_send()

    @pl.loop(0, count_gx * count_gy)
    def _(other):
        @pl.when(other != me)
        def _():
            pltpu.make_async_remote_copy(
                src_ref=estimate.at[0],
                dst_ref=cleaned.at[other],
                send_sem=plane_send.at[0],
                recv_sem=plane_recv.at[other],
                device_id=(gx, gy),
                device_id_type=MESH,
            ).wait_recv()

    def edge_copy(slot, up):
        target_pair, target_gy = device_of(count_gy, line + (1 if up else -1))
        source = cells if up else edge
        target = 0 if up else edge + cells
        side = 1 if up else 0
        return pltpu.make_async_remote_copy(
            src_ref=wide.at[slot, :, pl.ds(source, edge), :],
            dst_ref=wide.at[slot, :, pl.ds(target, edge), :],
            send_sem=send_sem.at[slot, side],
            recv_sem=recv_sem.at[slot, side],
            device_id=(target_pair * 2 + core, target_gy),
            device_id_type=MESH,
        )

    def planes_and_rows(field, slot, way, group):
        start = pl.multiple_of(group * SUB, SUB)
        value = field[:, pl.ds(start, SUB), :].reshape(size, width)
        value = jnp.dot(depth[way], split(value), preferred_element_type=jnp.float32)
        value = value[:size] + value[size:]
        value = value[:, :width] + value[:, width:]
        value = jnp.dot(split(value), rows[way], preferred_element_type=jnp.float32)
        value = value[:, :width] + value[:, width:]
        wide[slot, :, pl.ds(edge + start, SUB), :] = value.reshape(planes, SUB, width)

    inner = cells - 2 * edge

    def along_middle(slot, way, plane):
        value = split(wide[slot, plane, edge : edge + cells])
        value = jnp.dot(middle[way], value, preferred_element_type=jnp.float32)
        value = value[:inner] + value[inner:]
        return value[:, :width] + value[:, width:]

    def along_ends(slot, way, plane):
        low = wide[slot, plane, 0 : 3 * edge]
        high = wide[slot, plane, cells - edge : cells + 2 * edge]
        value = split(jnp.concatenate([low, high], axis=1))
        value = jnp.dot(ends[way], value, preferred_element_type=jnp.float32)
        value = value[:edge] + value[edge:]
        value = value[:, : 2 * width] + value[:, 2 * width :]
        return value[:, :width], value[:, width:]

    unroll = 4 if size <= 256 else 1
    groups = cells // SUB
    outer = edge // SUB

    def filter_ends(field, slot, way):
        @pl.loop(0, 2 * outer, unroll=4 if size <= 256 else 1)
        def _(step):
            planes_and_rows(field, slot, way, lax.rem(step + groups - outer, groups))

        @pl.when(line > 0)
        def _():
            edge_copy(slot, False).start()

        @pl.when(line < last)
        def _():
            edge_copy(slot, True).start()

    def filter_middle(field, slot, way):
        if inner:

            @pl.loop(outer, groups - outer, unroll=4 if size <= 256 and groups % 4 == 0 else 1)
            def _(group):
                planes_and_rows(field, slot, way, group)

    def wait_ends(slot):
        @pl.when(line > 0)
        def _():
            edge_copy(slot, False).wait_send()
            edge_copy(slot, True).wait_recv()

        @pl.when(line < last)
        def _():
            edge_copy(slot, True).wait_send()
            edge_copy(slot, False).wait_recv()

    def out_copy(chunk, target_gy):
        part = pl.ds(chunk * (planes // CHUNKS), planes // CHUNKS)
        return pltpu.make_async_remote_copy(
            src_ref=stage.at[target_gy, part],
            dst_ref=out.at[core, place % per_gx, part],
            send_sem=out_send.at[chunk, target_gy],
            recv_sem=out_recv.at[chunk, core, place % per_gx],
            device_id=(pair * 2 + place // per_gx, target_gy),
            device_id_type=MESH,
        )

    def own_copy(chunk):
        part = pl.ds(chunk * (planes // CHUNKS), planes // CHUNKS)
        return pltpu.make_async_copy(
            stage.at[gy, part], out.at[core, place % per_gx, part], own_sem.at[chunk]
        )

    def is_own(target_gy):
        return jnp.logical_and(target_gy == gy, place // per_gx == core)

    low_end = slice(0, edge)
    high_end = slice(cells - edge, cells)
    between = slice(edge, cells - edge)
    filter_ends(cleaned, 0, 0)
    for iteration in range(ITERS):
        source = cleaned if iteration == 0 else estimate
        filter_middle(source, 0, 0)
        if inner:

            @pl.loop(0, planes, unroll=unroll)
            def _(plane):
                blurred = along_middle(0, 0, plane) + BACKGROUND
                ratio[plane, between] = cleaned[plane, between] / blurred

        wait_ends(0)

        @pl.loop(0, planes, unroll=unroll)
        def _(plane):
            low, high = along_ends(0, 0, plane)
            ratio[plane, low_end] = cleaned[plane, low_end] / (low + BACKGROUND)
            ratio[plane, high_end] = cleaned[plane, high_end] / (high + BACKGROUND)

        filter_ends(ratio, 1, 1)
        filter_middle(ratio, 1, 1)
        if inner:

            @pl.loop(0, planes, unroll=unroll)
            def _(plane):
                estimate[plane, between] = source[plane, between] * along_middle(1, 1, plane)

        wait_ends(1)
        if iteration < ITERS - 1:

            @pl.loop(0, planes, unroll=unroll)
            def _(plane):
                low, high = along_ends(1, 1, plane)
                estimate[plane, low_end] = source[plane, low_end] * low
                estimate[plane, high_end] = source[plane, high_end] * high

            filter_ends(estimate, 0, 0)
        else:
            for chunk in range(CHUNKS):

                @pl.loop(chunk * (planes // CHUNKS), (chunk + 1) * (planes // CHUNKS), unroll=unroll)
                def _(plane):
                    low, high = along_ends(1, 1, plane)
                    pieces = [source[plane, low_end] * low]
                    if inner:
                        pieces.append(estimate[plane, between])
                    pieces.append(source[plane, high_end] * high)
                    value = jnp.concatenate(pieces, axis=0).T
                    for target in range(count_gy):
                        stage[target, plane] = value[target * lines_x : (target + 1) * lines_x]

                for target in range(count_gy):

                    @pl.when(is_own(target))
                    def _():
                        own_copy(chunk).start()

                    @pl.when(jnp.logical_not(is_own(target)))
                    def _():
                        out_copy(chunk, target).start()

    for chunk in range(CHUNKS):
        part = pl.ds(chunk * (planes // CHUNKS), planes // CHUNKS)
        for target in range(count_gy):

            @pl.when(is_own(target))
            def _():
                own_copy(chunk).wait()

            @pl.when(jnp.logical_not(is_own(target)))
            def _():
                out_copy(chunk, target).wait_send()

        for channel in range(2):
            for slot in range(per_gx):
                mine = jnp.logical_and(channel == core, place == core * per_gx + slot)

                @pl.when(jnp.logical_not(mine))
                def _():
                    pltpu.make_async_remote_copy(
                        src_ref=stage.at[0, part],
                        dst_ref=out.at[channel, slot, part],
                        send_sem=out_send.at[chunk, 0],
                        recv_sem=out_recv.at[chunk, channel, slot],
                        device_id=(gx, gy),
                        device_id_type=MESH,
                    ).wait_recv()


def local(raw_stack, psf_taps):
    channels, own_planes, lines_x, lines_y = raw_stack.shape
    half_taps = psf_taps.shape[2] // 2
    count_gx = lax.axis_size("gx")
    count_gy = lax.axis_size("gy")
    pairs = count_gx // channels
    cells = lines_y // (pairs * count_gy)
    planes = own_planes * count_gx * count_gy
    edge = -(-half_taps // SUB) * SUB

    block = min(lines_y, 256)
    size = planes * SUB
    per_gx = count_gy // 2
    block_x = lines_x // count_gy
    field = pltpu.VMEM((planes, cells, lines_x), jnp.float32)
    gathered = pl.pallas_call(
        functools.partial(deconvolve_kernel, count_gx, count_gy, edge),
        out_shape=jax.ShapeDtypeStruct((channels, per_gx, planes, block_x, cells), jnp.float32),
        in_specs=[pl.BlockSpec(memory_space=pl.ANY), pl.BlockSpec(memory_space=pltpu.SMEM)],
        out_specs=pl.BlockSpec(memory_space=pl.ANY),
        scratch_shapes=[
            field,
            field,
            field,
            pltpu.VMEM((2, planes, cells + 2 * edge, lines_x), jnp.float32),
            pltpu.VMEM((count_gy, planes, block_x, cells), jnp.float32),
            pltpu.VMEM((2 * block, lines_y), jnp.bfloat16),
            pltpu.VMEM((2 * lines_x, lines_y), jnp.bfloat16),
            pltpu.VMEM((2 * lines_x, lines_x), jnp.bfloat16),
            pltpu.VMEM((2, 2 * size, size), jnp.bfloat16),
            pltpu.VMEM((2, 2 * lines_x, 2 * lines_x), jnp.bfloat16),
            pltpu.VMEM((2, 2 * max(cells - 2 * edge, edge), cells), jnp.bfloat16),
            pltpu.VMEM((2, 2 * edge, 3 * edge), jnp.bfloat16),
            pltpu.VMEM((lines_x, lines_y), jnp.float32),
            pltpu.SemaphoreType.DMA((2, 2)),
            pltpu.SemaphoreType.DMA((2, 2)),
            pltpu.SemaphoreType.DMA((CHUNKS, count_gy)),
            pltpu.SemaphoreType.DMA((CHUNKS, channels, per_gx)),
            pltpu.SemaphoreType.DMA((CHUNKS,)),
            pltpu.SemaphoreType.DMA((planes,)),
            pltpu.SemaphoreType.DMA((planes,)),
            pltpu.SemaphoreType.DMA,
        ],
        compiler_params=pltpu.CompilerParams(
            collective_id=0, has_side_effects=True, vmem_limit_bytes=67043328
        ),
    )(raw_stack, psf_taps)
    return jnp.transpose(gathered, (0, 2, 3, 1, 4)).reshape(
        channels, planes, block_x, per_gx * cells
    )


def solution(mesh):
    in_specs = (P(None, ("gx", "gy"), None, None), P())
    out_specs = P(None, None, "gy", "gx")
    return jax.shard_map(local, mesh=mesh, in_specs=in_specs, out_specs=out_specs, check_vma=False)
```

```python
import functools

import jax
import jax.numpy as jnp
from jax import lax
from jax.experimental import pallas as pl
from jax.experimental.pallas import tpu as pltpu
from jax.sharding import PartitionSpec as P

ITERS = 2
BACKGROUND = 0.5
SIGMA_ACROSS = 48.0
SIGMA_ALONG = 96.0
SUB = 8
CHUNKS = 4
MESH = pl.DeviceIdType.MESH


def smoothing_table(length_cells, spread_cells):
    rows = lax.broadcasted_iota(jnp.int32, (length_cells, length_cells), 0)
    columns = lax.broadcasted_iota(jnp.int32, (length_cells, length_cells), 1)
    scaled = (rows - columns).astype(jnp.float32) / spread_cells
    kernel_table = jnp.exp(-0.5 * scaled * scaled)
    return kernel_table / jnp.sum(kernel_table, axis=1, keepdims=True)


def circular_row(length_cells, spread_cells):
    places = lax.broadcasted_iota(jnp.int32, (1, length_cells), 1)
    scaled = jnp.minimum(places, length_cells - places).astype(jnp.float32) / spread_cells
    kernel_row = jnp.exp(-0.5 * scaled * scaled)
    return kernel_row / jnp.sum(kernel_row, axis=1, keepdims=True)


def base_rows(taps, axis, channel, reach, lag_of):
    count = taps.shape[2]
    width = -(-2 * reach // 128) * 128
    place = lax.broadcasted_iota(jnp.int32, (1, width), 1)
    lag = lag_of(jnp.where(place < width // 2, place, place - width))
    forward = jnp.zeros((1, width), jnp.float32)
    backward = forward
    total = forward
    for k in range(count):
        tap = taps[axis, channel, k]
        total = total + tap
        forward = jnp.where(lag == k, tap, forward)
        backward = jnp.where(lag == count - 1 - k, tap, backward)
    return forward / total, backward / total


def shifted(base, start, count, columns):
    block = jnp.broadcast_to(base, (count, base.shape[1]))
    block = pltpu.roll(block, start, 1, stride=1, stride_axis=0)[:, :columns]
    high = block.astype(jnp.bfloat16)
    return high, (block - high.astype(jnp.float32)).astype(jnp.bfloat16)


def fill_tables(taps, channel, edge, cells, depth, rows, middle, ends):
    size, width = depth.shape[2], rows.shape[1] // 2
    half = taps.shape[2] // 2
    depth_base = base_rows(
        taps, 0, channel, size,
        lambda d: jnp.where((d & (SUB - 1)) == 0, (d >> (SUB.bit_length() - 1)) + half, -1),
    )
    rows_base = base_rows(taps, 1, channel, width, lambda d: half - d)
    lines_base = base_rows(taps, 2, channel, max(cells, 3 * edge), lambda d: d - edge + half)
    for way in range(2):
        for start in range(0, size, 256):
            high, low = shifted(depth_base[way], start, min(256, size), size)
            depth[way, pl.ds(start, high.shape[0])] = high
            depth[way, pl.ds(size + start, high.shape[0])] = low
        high, low = shifted(rows_base[way], 0, width, width)
        both = jnp.concatenate([high, low], axis=1)
        rows[way] = jnp.concatenate([both, both], axis=0)
        if cells > 2 * edge:
            high, low = shifted(lines_base[way], 0, cells - 2 * edge, cells)
            middle[way] = jnp.concatenate([high, low], axis=0)
        high, low = shifted(lines_base[way], 0, edge, 3 * edge)
        ends[way] = jnp.concatenate([high, low], axis=0)


def split(value):
    high = value.astype(jnp.bfloat16)
    low = (value - high.astype(jnp.float32)).astype(jnp.bfloat16)
    return jnp.concatenate([high, low], axis=1)


def place_of(count_gy, pair, gy):
    first = gy // 2
    along = 2 * first + (gy % 2 + first) % 2
    odd = pair % 2
    return (1 - odd) * along + odd * (count_gy - 1 - along)


def device_of(count_gy, line):
    pair, place = line // count_gy, line % count_gy
    odd = pair % 2
    along = (1 - odd) * place + odd * (count_gy - 1 - place)
    first = along // 2
    return pair, 2 * first + (along % 2 + first) % 2


def deconvolve_kernel(
    count_gx, count_gy, edge, raw, taps, out,
    cleaned, estimate, ratio, wide, stage, along, smooth, across, depth, rows, middle, ends,
    held, send_sem, recv_sem, out_send, out_recv, own_sem, plane_send, plane_recv, held_sem,
):
    planes, cells, width = cleaned.shape
    size = planes * SUB
    gx, gy = lax.axis_index("gx"), lax.axis_index("gy")
    pair, core = gx // 2, gx % 2
    place = place_of(count_gy, pair, gy)
    line = pair * count_gy + place
    last = count_gx // 2 * count_gy - 1
    per_gx = count_gy // 2
    lines_x = width // count_gy
    me = gx * count_gy + gy

    def load(channel):
        return pltpu.make_async_copy(raw.at[channel, 0], held, held_sem)

    load(0).start()
    barrier = pltpu.get_barrier_semaphore()

    @pl.loop(0, count_gx * count_gy)
    def _(other):
        @pl.when(other != me)
        def _():
            pl.semaphore_signal(
                barrier, inc=1, device_id=(other // count_gy, other % count_gy), device_id_type=MESH
            )

    channels, _, _, lines_y = raw.shape
    block = along.shape[0] // 2
    blocks = lines_y // block
    chunks = lines_y // cells
    per_block = block // cells
    table = smoothing_table(width, SIGMA_ACROSS)
    high = table.astype(jnp.bfloat16)
    across[0:width] = high
    across[width : 2 * width] = (table - high.astype(jnp.float32)).astype(jnp.bfloat16)
    high, low = shifted(circular_row(lines_y, SIGMA_ALONG), 0, block, lines_y)
    along[0:block] = high
    along[block : 2 * block] = low

    def smooth_block(index):
        columns = pl.ds(pl.multiple_of(index * block, block), block)
        value = held[:, columns]
        high = value.astype(jnp.bfloat16)
        low = (value - high.astype(jnp.float32)).astype(jnp.bfloat16)
        product = jnp.dot(across[...], high, preferred_element_type=jnp.float32)
        total = product[:width] + product[width:]
        total += jnp.dot(across[0:width], low, preferred_element_type=jnp.float32)
        high = total.astype(jnp.bfloat16)
        smooth[0:width, columns] = high
        smooth[width : 2 * width, columns] = (total - high.astype(jnp.float32)).astype(jnp.bfloat16)

    def clean_block(channel, index):
        total = jnp.zeros((width, block), jnp.float32)
        for other in range(blocks):
            columns = pl.ds(other * block, block)
            shift = lax.rem(index - other + blocks, blocks)
            table = pl.ds(pl.multiple_of(shift * block, block), block)
            product = jnp.dot(
                smooth[:, columns], along[0:block, table], preferred_element_type=jnp.float32
            )
            total += product[:width] + product[width:]
            total += jnp.dot(
                smooth[0:width, columns], along[block : 2 * block, table],
                preferred_element_type=jnp.float32,
            )
        columns = pl.ds(pl.multiple_of(index * block, block), block)
        smoothed = smooth[0:width, columns].astype(jnp.float32)
        smoothed += smooth[width : 2 * width, columns].astype(jnp.float32)
        value = jnp.maximum(held[:, columns] - (smoothed - total), 0.0)
        estimate[pl.ds(channel * chunks + index * per_block, per_block)] = value.T.reshape(
            per_block, cells, width
        )

    def plane_copy(channel, chunk):
        target_pair, target_gy = device_of(count_gy, chunk)
        return pltpu.make_async_remote_copy(
            src_ref=estimate.at[channel * chunks + chunk],
            dst_ref=cleaned.at[me],
            send_sem=plane_send.at[channel * chunks + chunk],
            recv_sem=plane_recv.at[me],
            device_id=(target_pair * 2 + channel, target_gy),
            device_id_type=MESH,
        )

    own_plane = pltpu.make_async_copy(
        estimate.at[core * chunks + line], cleaned.at[me], plane_send.at[core * chunks + line]
    )

    def is_own_plane(channel, chunk):
        return jnp.logical_and(channel == core, chunk == line)

    for channel in range(channels):
        if channel > 0:
            load(channel).start()
        load(channel).wait()

        @pl.loop(0, blocks, unroll=2)
        def _(index):
            smooth_block(index)

        if channel == 0:
            pl.semaphore_wait(barrier, count_gx * count_gy - 1)

        @pl.loop(0, blocks)
        def _(step):
            index = lax.rem(step + (line + 1) // per_block + blocks // 2, blocks)
            clean_block(channel, index)
            for part in range(per_block):
                chunk = index * per_block + part

                @pl.when(is_own_plane(channel, chunk))
                def _():
                    own_plane.start()

                @pl.when(jnp.logical_not(is_own_plane(channel, chunk)))
                def _():
                    plane_copy(channel, chunk).start()

    fill_tables(taps, core, edge, cells, depth, rows, middle, ends)

    zeros = jnp.zeros((planes, edge, width), jnp.float32)

    @pl.when(line == 0)
    def _():
        for slot in range(2):
            wide[slot, :, 0:edge, :] = zeros

    @pl.when(line == last)
    def _():
        for slot in range(2):
            wide[slot, :, edge + cells :, :] = zeros

    own_plane.wait()
    for channel in range(channels):

        @pl.loop(0, chunks)
        def _(chunk):
            @pl.when(jnp.logical_not(is_own_plane(channel, chunk)))
            def _():
                plane_copy(channel, chunk).wait_send()

    @pl.loop(0, count_gx * count_gy)
    def _(other):
        @pl.when(other != me)
        def _():
            pltpu.make_async_remote_copy(
                src_ref=estimate.at[0],
                dst_ref=cleaned.at[other],
                send_sem=plane_send.at[0],
                recv_sem=plane_recv.at[other],
                device_id=(gx, gy),
                device_id_type=MESH,
            ).wait_recv()

    def edge_copy(slot, up):
        target_pair, target_gy = device_of(count_gy, line + (1 if up else -1))
        source = cells if up else edge
        target = 0 if up else edge + cells
        side = 1 if up else 0
        return pltpu.make_async_remote_copy(
            src_ref=wide.at[slot, :, pl.ds(source, edge), :],
            dst_ref=wide.at[slot, :, pl.ds(target, edge), :],
            send_sem=send_sem.at[slot, side],
            recv_sem=recv_sem.at[slot, side],
            device_id=(target_pair * 2 + core, target_gy),
            device_id_type=MESH,
        )

    def planes_and_rows(field, slot, way, group):
        start = pl.multiple_of(group * SUB, SUB)
        value = field[:, pl.ds(start, SUB), :].reshape(size, width)
        value = jnp.dot(depth[way], split(value), preferred_element_type=jnp.float32)
        value = value[:size] + value[size:]
        value = value[:, :width] + value[:, width:]
        value = jnp.dot(split(value), rows[way], preferred_element_type=jnp.float32)
        value = value[:, :width] + value[:, width:]
        wide[slot, :, pl.ds(edge + start, SUB), :] = value.reshape(planes, SUB, width)

    inner = cells - 2 * edge

    def along_middle(slot, way, plane):
        value = split(wide[slot, plane, edge : edge + cells])
        value = jnp.dot(middle[way], value, preferred_element_type=jnp.float32)
        value = value[:inner] + value[inner:]
        return value[:, :width] + value[:, width:]

    def along_ends(slot, way, plane):
        low = wide[slot, plane, 0 : 3 * edge]
        high = wide[slot, plane, cells - edge : cells + 2 * edge]
        value = split(jnp.concatenate([low, high], axis=1))
        value = jnp.dot(ends[way], value, preferred_element_type=jnp.float32)
        value = value[:edge] + value[edge:]
        value = value[:, : 2 * width] + value[:, 2 * width :]
        return value[:, :width], value[:, width:]

    unroll = 8 if size <= 256 else 1
    groups = cells // SUB
    outer = edge // SUB

    def filter_ends(field, slot, way):
        @pl.loop(0, 2 * outer, unroll=4 if size <= 256 else 1)
        def _(step):
            planes_and_rows(field, slot, way, lax.rem(step + groups - outer, groups))

        @pl.when(line > 0)
        def _():
            edge_copy(slot, False).start()

        @pl.when(line < last)
        def _():
            edge_copy(slot, True).start()

    def filter_middle(field, slot, way):
        if inner:

            @pl.loop(outer, groups - outer, unroll=4 if size <= 256 and groups % 4 == 0 else 1)
            def _(group):
                planes_and_rows(field, slot, way, group)

    def wait_ends(slot):
        @pl.when(line > 0)
        def _():
            edge_copy(slot, False).wait_send()
            edge_copy(slot, True).wait_recv()

        @pl.when(line < last)
        def _():
            edge_copy(slot, True).wait_send()
            edge_copy(slot, False).wait_recv()

    def out_copy(chunk, target_gy):
        part = pl.ds(chunk * (planes // CHUNKS), planes // CHUNKS)
        return pltpu.make_async_remote_copy(
            src_ref=stage.at[target_gy, part],
            dst_ref=out.at[core, place % per_gx, part],
            send_sem=out_send.at[chunk, target_gy],
            recv_sem=out_recv.at[chunk, core, place % per_gx],
            device_id=(pair * 2 + place // per_gx, target_gy),
            device_id_type=MESH,
        )

    def own_copy(chunk):
        part = pl.ds(chunk * (planes // CHUNKS), planes // CHUNKS)
        return pltpu.make_async_copy(
            stage.at[gy, part], out.at[core, place % per_gx, part], own_sem.at[chunk]
        )

    def is_own(target_gy):
        return jnp.logical_and(target_gy == gy, place // per_gx == core)

    low_end = slice(0, edge)
    high_end = slice(cells - edge, cells)
    between = slice(edge, cells - edge)
    filter_ends(cleaned, 0, 0)
    for iteration in range(ITERS):
        source = cleaned if iteration == 0 else estimate
        filter_middle(source, 0, 0)
        if inner:

            @pl.loop(0, planes, unroll=unroll)
            def _(plane):
                blurred = along_middle(0, 0, plane) + BACKGROUND
                ratio[plane, between] = cleaned[plane, between] / blurred

        wait_ends(0)

        @pl.loop(0, planes, unroll=unroll)
        def _(plane):
            low, high = along_ends(0, 0, plane)
            ratio[plane, low_end] = cleaned[plane, low_end] / (low + BACKGROUND)
            ratio[plane, high_end] = cleaned[plane, high_end] / (high + BACKGROUND)

        filter_ends(ratio, 1, 1)
        filter_middle(ratio, 1, 1)
        if inner:

            @pl.loop(0, planes, unroll=unroll)
            def _(plane):
                estimate[plane, between] = source[plane, between] * along_middle(1, 1, plane)

        wait_ends(1)
        if iteration < ITERS - 1:

            @pl.loop(0, planes, unroll=unroll)
            def _(plane):
                low, high = along_ends(1, 1, plane)
                estimate[plane, low_end] = source[plane, low_end] * low
                estimate[plane, high_end] = source[plane, high_end] * high

            filter_ends(estimate, 0, 0)
        else:
            for chunk in range(CHUNKS):

                @pl.loop(chunk * (planes // CHUNKS), (chunk + 1) * (planes // CHUNKS), unroll=unroll)
                def _(plane):
                    low, high = along_ends(1, 1, plane)
                    pieces = [source[plane, low_end] * low]
                    if inner:
                        pieces.append(estimate[plane, between])
                    pieces.append(source[plane, high_end] * high)
                    value = jnp.concatenate(pieces, axis=0).T
                    for target in range(count_gy):
                        stage[target, plane] = value[target * lines_x : (target + 1) * lines_x]

                for step in range(count_gy):
                    target = lax.rem(gy + 1 + step, count_gy)

                    @pl.when(is_own(target))
                    def _():
                        own_copy(chunk).start()

                    @pl.when(jnp.logical_not(is_own(target)))
                    def _():
                        out_copy(chunk, target).start()

    for chunk in range(CHUNKS):
        part = pl.ds(chunk * (planes // CHUNKS), planes // CHUNKS)
        for target in range(count_gy):

            @pl.when(is_own(target))
            def _():
                own_copy(chunk).wait()

            @pl.when(jnp.logical_not(is_own(target)))
            def _():
                out_copy(chunk, target).wait_send()

        for channel in range(2):
            for slot in range(per_gx):
                mine = jnp.logical_and(channel == core, place == core * per_gx + slot)

                @pl.when(jnp.logical_not(mine))
                def _():
                    pltpu.make_async_remote_copy(
                        src_ref=stage.at[0, part],
                        dst_ref=out.at[channel, slot, part],
                        send_sem=out_send.at[chunk, 0],
                        recv_sem=out_recv.at[chunk, channel, slot],
                        device_id=(gx, gy),
                        device_id_type=MESH,
                    ).wait_recv()


def local(raw_stack, psf_taps):
    channels, own_planes, lines_x, lines_y = raw_stack.shape
    half_taps = psf_taps.shape[2] // 2
    count_gx = lax.axis_size("gx")
    count_gy = lax.axis_size("gy")
    pairs = count_gx // channels
    cells = lines_y // (pairs * count_gy)
    planes = own_planes * count_gx * count_gy
    edge = -(-half_taps // SUB) * SUB

    block = min(lines_y, 256)
    size = planes * SUB
    per_gx = count_gy // 2
    block_x = lines_x // count_gy
    field = pltpu.VMEM((planes, cells, lines_x), jnp.float32)
    gathered = pl.pallas_call(
        functools.partial(deconvolve_kernel, count_gx, count_gy, edge),
        out_shape=jax.ShapeDtypeStruct((channels, per_gx, planes, block_x, cells), jnp.float32),
        in_specs=[pl.BlockSpec(memory_space=pl.ANY), pl.BlockSpec(memory_space=pltpu.SMEM)],
        out_specs=pl.BlockSpec(memory_space=pl.ANY),
        scratch_shapes=[
            field,
            field,
            field,
            pltpu.VMEM((2, planes, cells + 2 * edge, lines_x), jnp.float32),
            pltpu.VMEM((count_gy, planes, block_x, cells), jnp.float32),
            pltpu.VMEM((2 * block, lines_y), jnp.bfloat16),
            pltpu.VMEM((2 * lines_x, lines_y), jnp.bfloat16),
            pltpu.VMEM((2 * lines_x, lines_x), jnp.bfloat16),
            pltpu.VMEM((2, 2 * size, size), jnp.bfloat16),
            pltpu.VMEM((2, 2 * lines_x, 2 * lines_x), jnp.bfloat16),
            pltpu.VMEM((2, 2 * max(cells - 2 * edge, edge), cells), jnp.bfloat16),
            pltpu.VMEM((2, 2 * edge, 3 * edge), jnp.bfloat16),
            pltpu.VMEM((lines_x, lines_y), jnp.float32),
            pltpu.SemaphoreType.DMA((2, 2)),
            pltpu.SemaphoreType.DMA((2, 2)),
            pltpu.SemaphoreType.DMA((CHUNKS, count_gy)),
            pltpu.SemaphoreType.DMA((CHUNKS, channels, per_gx)),
            pltpu.SemaphoreType.DMA((CHUNKS,)),
            pltpu.SemaphoreType.DMA((planes,)),
            pltpu.SemaphoreType.DMA((planes,)),
            pltpu.SemaphoreType.DMA,
        ],
        compiler_params=pltpu.CompilerParams(
            collective_id=0, has_side_effects=True, vmem_limit_bytes=67043328
        ),
    )(raw_stack, psf_taps)
    return jnp.transpose(gathered, (0, 2, 3, 1, 4)).reshape(
        channels, planes, block_x, per_gx * cells
    )


def solution(mesh):
    in_specs = (P(None, ("gx", "gy"), None, None), P())
    out_specs = P(None, None, "gy", "gx")
    return jax.shard_map(local, mesh=mesh, in_specs=in_specs, out_specs=out_specs, check_vma=False)
```
